32 devices in a mesh: expert: 8 (over z, x), mp: 4 (over y, core).
Axes of the slice: x: 2, y: 2, z: 4, core: 2. Of those that a mesh axis runs over, the one named last changes fastest.
Arguments:
- routes: int32 [1024, 8], P('expert'), may hold values from 0 to 15, all different within a row; in each aligned block of 128 rows (0 to 127, 128 to 255, ...) at most 96 rows name the same one
- routed_hidden: bfloat16 [1024, 8, 1024], P('expert', None, 'mp'), may hold values from -36 to 36
- down_proj: bfloat16 [16, 1024, 3584], P('expert', None, 'mp'), may hold values from -6 to 6
- merge_group: int32 [16], replicated, may hold values from 0 to 7, as said below
Outputs:
- merged: bfloat16 [8, 1024, 3584], P('expert', None, 'mp')
The draws below stay inside these ranges and needn't reach their ends.
Inputs may be any that keep to these rules, and one draw needn't show every extreme that they name: `routes`: among the 128 tokens of one index of the expert axis (aligned blocks of rows) no expert is named more than 96 times, a bound that some block reaches. `merge_group`: every group holds 1 to 3 experts, and some group holds exactly 3.
All inputs are finite; a program needn't handle non-finite values.
Results may differ from the reference program's by a relative error of at most 0.0056.
Values may be sent and summed in bfloat16 or wider, within the bound.
A program may use at most 128 MiB of HBM per device.

```python
import math
import jax
import jax.numpy as jnp
import numpy as np
from jax import lax

FF = 1024
DW = 3584
TOP = 8
GMAX = 3
TOK_DEV = 128
EXPERTS = 16
GROUPS = 8
TOKENS = 1024
CAP = 96
SLOTS = 768


def draw_routed_hidden(key, part):
    col_key, row_key, base_key = jax.random.split(jax.random.fold_in(key, 17), 3)
    log_lower = math.log(0.3)
    log_upper = math.log(3.0)
    col_scale = jnp.exp(jax.random.uniform(col_key, (FF,), jnp.float32, log_lower, log_upper))
    row_scale = jnp.exp(jax.random.uniform(row_key, (TOKENS, TOP, 1), jnp.float32, log_lower, log_upper))
    base_values = jnp.clip(jax.random.normal(base_key, (TOKENS, TOP, FF), jnp.float32), -4.0, 4.0)
    return (base_values * row_scale * col_scale[None, None, :]).astype(jnp.bfloat16)


def draw_merge_group(key, part):
    kind_key, first_key, shuffle_key = jax.random.split(jax.random.fold_in(key, 29), 3)
    pair_kind = jax.random.randint(kind_key, (GROUPS // 2,), 0, GMAX)
    pair_kind = pair_kind.at[0].set((GMAX - 1) * jax.random.randint(first_key, (), 0, 2))
    group_sizes = jnp.stack([pair_kind + 1, GMAX - pair_kind], axis=1).reshape(GROUPS)
    bounds = jnp.cumsum(group_sizes)
    labels = jnp.sum((bounds[None, :] <= jnp.arange(EXPERTS)[:, None]).astype(jnp.int32), axis=1)
    shuffle = jax.random.permutation(shuffle_key, EXPERTS)
    return labels[shuffle].astype(jnp.int32)


def level_of(rng, shape, cuts, least, top_value):
    gain, own = 1.0, jax.random.fold_in(rng, 6)
    for axis_at, shards_of in cuts:
        draws = jnp.exp(jax.random.uniform(jax.random.fold_in(own, axis_at), (shards_of,), jnp.float32, least / len(cuts), top_value / len(cuts)))
        gain = gain * jnp.repeat(draws, shape[axis_at] // shards_of).reshape([-1 if axis == axis_at else 1 for axis in range(len(shape))])
    return gain


def routed_block(key, own, number, rows, amount, top, bound, slope):
    ranking = jax.random.permutation(key, amount)
    crowded, usual = portions_of(amount, rows * top, bound, slope, True), portions_of(amount, rows * top, bound, slope, False)
    places = jnp.arange(amount)

    def named(tallies, offset_by):
        used = int((tallies > 0).sum())
        fixed = max(1, used // 4)
        passed = fixed + (places - fixed + offset_by * (used - fixed)) % max(1, amount - fixed)
        return jnp.zeros((amount,), jnp.int32).at[ranking[jnp.where(places < fixed, places, passed)]].set(jnp.asarray(tallies, jnp.int32))

    tallies = jnp.where(number % 4 == 0, named(crowded, number // 4), named(usual, number - number // 4 - 1))
    mixed = jax.random.permutation(jax.random.fold_in(own, 3), amount)
    giver, receiver = mixed[0:amount // 2 * 2:2], mixed[1:amount // 2 * 2:2]
    margin = jnp.minimum(tallies[giver] - 1, bound - tallies[receiver]) // 2
    margin = jnp.where((giver == ranking[0]) | (receiver == ranking[0]) | (tallies[receiver] == 0), 0, jnp.maximum(margin, 0))
    passed = jax.random.randint(jax.random.fold_in(own, 4), (amount // 2,), 0, 1 << 20) % (margin + 1)
    tallies = tallies.at[giver].add(-passed).at[receiver].add(passed)
    items = jnp.searchsorted(jnp.cumsum(tallies), jnp.arange(rows * top), side="right").astype(jnp.int32)
    listing = items.reshape(top, rows).T
    listing = listing[jax.random.permutation(jax.random.fold_in(own, 1), rows)]
    offset_by = jax.random.randint(jax.random.fold_in(own, 2), (rows, 1), 0, top)
    return jnp.take_along_axis(listing, (jnp.arange(top)[None, :] + offset_by) % top, axis=1)


def portions_of(count, total, bound, lean, full):
    weights = [(1 << 20) // math.isqrt(standing ** lean) + 1 for standing in range(1, count + 1)]
    largest = bound if full else min(bound, max(-(-total // count), total * weights[0] // sum(weights)))
    least = 1 if total - largest >= count - 1 else 0
    holding, surplus = [largest] + [least] * (count - 1), total - largest - least * (count - 1)
    while surplus > 0:
        candidates = [i for i in range(1, count) if holding[i] < largest] or [i for i in range(1, count) if holding[i] < bound]
        whole, left = sum([weights[i] for i in candidates]), surplus
        for i in candidates:
            addition = min(bound - holding[i], max(1, left * weights[i] // whole), surplus)
            holding[i] = holding[i] + addition
            surplus = surplus - addition
    return np.array(holding)


def centred(rng, extent, width, limit, shards=(), kind=jnp.bfloat16):
    values = jax.random.normal(rng, extent, jnp.float32) * width
    if len(shards) > 0:
        values = level_of(rng, extent, shards, -0.22, 0.18) * values
    return jnp.clip(values, min=-limit, max=limit).astype(kind)


def setup_inputs(seed: int = 0) -> dict:
    key_of = jax.random.split(jax.random.key(seed), 5)
    routes_keys = jax.random.split(jax.random.fold_in(key_of[0], 1), TOKENS // TOK_DEV)
    routes_turns = jax.random.permutation(jax.random.fold_in(key_of[0], 3), TOKENS // TOK_DEV)
    routes = jax.vmap(lambda own, number: routed_block(jax.random.fold_in(key_of[0], 2), own, number, TOK_DEV, EXPERTS, TOP, CAP, 2))(routes_keys, routes_turns).reshape((TOKENS, TOP))
    routed_hidden = draw_routed_hidden(jax.random.fold_in(key_of[4], 71), 0)
    down_proj = centred(key_of[2], (EXPERTS, FF, DW), 1.0, 6.0, ((0, 8), (2, 4)))
    merge_group = draw_merge_group(jax.random.fold_in(key_of[4], 71), 0)
    return {"routes": routes, "routed_hidden": routed_hidden, "down_proj": down_proj, "merge_group": merge_group}


damping = 0.1
epsilon = 1e-05

def slot_rank(labels, label_count):
    onehot = (labels[:, None] == jnp.arange(label_count, dtype=jnp.int32)[None, :]).astype(jnp.int32)
    return jnp.sum(onehot * (jnp.cumsum(onehot, axis=0) - 1), axis=1).astype(jnp.int32)

def member_table(merge_group, group_count):
    expert_total = merge_group.shape[0]
    position = slot_rank(merge_group, group_count)
    slot_table = jnp.full((group_count * GMAX,), -1, jnp.int32)
    slot_table = slot_table.at[merge_group * GMAX + position].set(jnp.arange(expert_total, dtype=jnp.int32))
    return slot_table.reshape(group_count, GMAX)

def solve_group(gram_sum, partial_value):
    order_size = gram_sum.shape[0]
    ridge_term = damping * jnp.trace(gram_sum) / order_size + epsilon
    system = gram_sum + ridge_term * jnp.eye(order_size, dtype=jnp.float32)
    factor = jnp.linalg.cholesky(system)
    return jax.scipy.linalg.cho_solve((factor, True), partial_value)

def reference(routes, routed_hidden, down_proj, merge_group):
    row_count = TOKENS * TOP
    targets = routes.reshape(row_count).astype(jnp.int32)
    padded = jnp.concatenate([routed_hidden.reshape(row_count, FF), jnp.zeros((1, FF), routed_hidden.dtype)], axis=0)
    sorted_rows = jnp.argsort(targets, stable=True).astype(jnp.int32)
    counts = jnp.zeros((EXPERTS,), jnp.int32).at[targets].add(1)
    starts = jnp.cumsum(counts).astype(jnp.int32) - counts
    places = jnp.arange(SLOTS, dtype=jnp.int32)
    members = member_table(merge_group.astype(jnp.int32), GROUPS)
    highest = lax.Precision.HIGHEST

    def expert_terms(expert):
        position = starts[expert] + places
        valid_slot = places < counts[expert]
        source_row = jnp.where(valid_slot, sorted_rows[jnp.minimum(position, row_count - 1)], row_count)
        expert_rows = padded[source_row].astype(jnp.float32)
        weight = down_proj[expert].astype(jnp.float32)
        gram_term = jnp.dot(expert_rows.T, expert_rows, precision=highest)
        projected = jnp.dot(expert_rows, weight, precision=highest)
        projected = lax.optimization_barrier(projected.astype(jnp.bfloat16)).astype(jnp.float32)
        product = jnp.dot(expert_rows.T, projected, precision=highest)
        return (gram_term, product)

    def empty_terms(expert):
        return (jnp.zeros((FF, FF), jnp.float32), jnp.zeros((FF, DW), jnp.float32))

    def merge_one(group_index):
        gram_sum = jnp.zeros((FF, FF), jnp.float32)
        partial_value = jnp.zeros((FF, DW), jnp.float32)
        for member_slot in range(GMAX):
            expert = members[group_index, member_slot]
            gram_term, product = lax.cond(expert >= 0, expert_terms, empty_terms, jnp.maximum(expert, 0))
            gram_sum = gram_sum + gram_term
            partial_value = partial_value + product
        return solve_group(gram_sum, partial_value).astype(jnp.bfloat16)
    return lax.map(merge_one, jnp.arange(GROUPS, dtype=jnp.int32))
```

```python
import jax
import jax.numpy as jnp
from jax import lax
from jax.experimental import pallas as pl
from jax.experimental.pallas import tpu as pltpu
from jax.sharding import PartitionSpec as P

GMAX = 3
BLOCK = 128
PANEL = 8

damping = 0.1
epsilon = 1e-05
HIGHEST = lax.Precision.HIGHEST


def slot_rank(labels, label_count):
    count = labels.shape[0]
    onehot = labels[:, None] == jnp.arange(label_count, dtype=jnp.int32)[None, :]
    order = jnp.arange(count, dtype=jnp.int32)
    before = (order[None, :] < order[:, None]).astype(jnp.bfloat16)
    ahead = jnp.dot(before, onehot.astype(jnp.bfloat16), preferred_element_type=jnp.float32)
    return jnp.sum(jnp.where(onehot, ahead, 0.0), axis=1).astype(jnp.int32)


def invert_small(entry):
    size = len(entry)
    value = {(i, j): entry[i][j] for i in range(size) for j in range(i, size)}

    def get(i, j):
        return value[(min(i, j), max(i, j))]

    for k in range(0, size, 2):
        a, b, d = get(k, k), get(k, k + 1), get(k + 1, k + 1)
        scale = 1.0 / (a * d - b * b)
        a, b, d = a * scale, b * scale, d * scale
        others = [i for i in range(size) if i not in (k, k + 1)]
        scaled = {
            i: (get(i, k) * d - get(i, k + 1) * b, get(i, k + 1) * a - get(i, k) * b)
            for i in others
        }
        for i in others:
            for j in others:
                if i <= j:
                    value[(i, j)] = value[(i, j)] - (
                        scaled[i][0] * get(j, k) + scaled[i][1] * get(j, k + 1)
                    )
        for i in others:
            value[(min(i, k), max(i, k))] = scaled[i][0]
            value[(min(i, k + 1), max(i, k + 1))] = scaled[i][1]
        value[(k, k)], value[(k, k + 1)], value[(k + 1, k + 1)] = -d, b, -a
    return [[-get(i, j) for j in range(size)] for i in range(size)]


def tree_sum(terms):
    while len(terms) > 1:
        terms = [sum(terms[i : i + 2][1:], terms[i]) for i in range(0, len(terms), 2)]
    return terms[0]


def invert_tile(tile_ref):
    size = tile_ref.shape[0]
    full = (PANEL, size)
    lane = lax.broadcasted_iota(jnp.int32, full, 1)
    sub = lax.broadcasted_iota(jnp.int32, full, 0)
    panels = size // PANEL
    group = [tile_ref[g * PANEL : (g + 1) * PANEL, :] for g in range(panels)]
    for p in range(panels):
        first = p * PANEL
        columns = [jnp.broadcast_to(group[p][:, first + j : first + j + 1], full) for j in range(PANEL)]
        entry = [
            [jnp.broadcast_to(columns[j][i : i + 1, :], full) for j in range(PANEL)]
            for i in range(PANEL)
        ]
        inverse = invert_small(entry)
        own = [inverse[0][j] for j in range(PANEL)]
        for i in range(1, PANEL):
            own = [jnp.where(sub == i, inverse[i][j], own[j]) for j in range(PANEL)]
        row = [jnp.broadcast_to(group[p][j : j + 1, :], full) for j in range(PANEL)]
        scaled = tree_sum([own[j] * row[j] for j in range(PANEL)])
        for j in range(PANEL):
            scaled = jnp.where(lane == first + j, own[j], scaled)
        spread = [jnp.broadcast_to(scaled[j : j + 1, :], full) for j in range(PANEL)]
        pivots = (lane >= first) & (lane < first + PANEL)
        order = [(p + 1 + g) % panels for g in range(panels - 1)]
        for g in order:
            here = group[g]
            group[g] = jnp.where(pivots, 0.0, here) - tree_sum(
                [
                    jnp.broadcast_to(here[:, first + j : first + j + 1], full) * spread[j]
                    for j in range(PANEL)
                ]
            )
        group[p] = scaled
    for g in range(panels):
        tile_ref[g * PANEL : (g + 1) * PANEL, :] = group[g]


def inverse_kernel(a_ref, o_ref, s_ref, d_ref):
    size = a_ref.shape[0]
    o_ref[...] = a_ref[...]
    tiles = size // BLOCK

    def eliminate(step, carry):
        span = pl.ds(pl.multiple_of(step * BLOCK, BLOCK), BLOCK)
        d_ref[...] = o_ref[span, span]
        invert_tile(d_ref)
        inverse = d_ref[...]
        s_ref[...] = jnp.dot(
            inverse, o_ref[span, :], precision=HIGHEST, preferred_element_type=jnp.float32
        )
        s_ref[:, span] = inverse

        def update(tile, inner):
            here = pl.ds(pl.multiple_of(tile * BLOCK, BLOCK), BLOCK)
            column = o_ref[here, span]
            o_ref[here, span] = jnp.zeros((BLOCK, BLOCK), jnp.float32)
            o_ref[here, :] = o_ref[here, :] - jnp.dot(
                column, s_ref[...], precision=HIGHEST, preferred_element_type=jnp.float32
            )
            return inner

        lax.fori_loop(0, tiles, update, 0)
        o_ref[span, :] = s_ref[...]
        return carry

    lax.fori_loop(0, tiles, eliminate, 0)


def spd_inverse(system):
    size = system.shape[0]
    return pl.pallas_call(
        inverse_kernel,
        out_shape=jax.ShapeDtypeStruct(system.shape, jnp.float32),
        in_specs=[pl.BlockSpec(memory_space=pltpu.VMEM)],
        out_specs=pl.BlockSpec(memory_space=pltpu.VMEM),
        scratch_shapes=[
            pltpu.VMEM((BLOCK, size), jnp.float32),
            pltpu.VMEM((BLOCK, BLOCK), jnp.float32),
        ],
        compiler_params=pltpu.CompilerParams(vmem_limit_bytes=24 << 20),
        cost_estimate=pl.CostEstimate(
            flops=50 * size**3, bytes_accessed=8 * size * size, transcendentals=0
        ),
    )(system)


def on_device(routes, routed_hidden, down_proj, merge_group):
    expert_count = lax.axis_size("expert")
    local_count = down_proj.shape[0]
    expert_total = local_count * expert_count
    tok_count, top_count = routes.shape
    hidden_part = routed_hidden.shape[2]
    full_width = down_proj.shape[1]
    out_part = down_proj.shape[2]
    slot_cap = 3 * tok_count * top_count // (2 * expert_total)
    row_count = tok_count * top_count
    piece_rows = full_width // expert_count

    weight_pieces = down_proj.reshape(local_count, expert_count, piece_rows, out_part)
    weights_all = lax.all_to_all(weight_pieces, "expert", split_axis=1, concat_axis=1, tiled=True)

    experts = jnp.arange(expert_total, dtype=jnp.int32)
    member_rank = slot_rank(merge_group, expert_count)
    first_slot = (member_rank * expert_count + merge_group) * slot_cap
    targets = routes.reshape(row_count)
    position = slot_rank(targets, expert_total)
    slot_index = position + jnp.sum(
        jnp.where(targets[:, None] == experts[None, :], first_slot[None, :], 0), axis=1
    )
    slots = jnp.arange(GMAX * expert_count * slot_cap, dtype=jnp.int32)
    chosen = (slots[:, None] == slot_index[None, :]).astype(jnp.bfloat16)
    outgoing = jnp.dot(
        chosen,
        routed_hidden.reshape(row_count, hidden_part),
        preferred_element_type=jnp.float32,
    ).astype(jnp.bfloat16)
    outgoing = outgoing.reshape(GMAX, expert_count * slot_cap, hidden_part)
    arrived = lax.all_to_all(outgoing, "expert", split_axis=1, concat_axis=1, tiled=True)
    rows = lax.all_gather(arrived, "mp", axis=2, tiled=True)

    table = jnp.arange(GMAX * expert_count, dtype=jnp.int32)
    place = member_rank * expert_count + merge_group
    members = jnp.sum(jnp.where(table[:, None] == place[None, :], experts[None, :], 0), axis=1)
    picked = weights_all.reshape(expert_total, piece_rows, out_part)[
        (members % local_count) * expert_count + members // local_count
    ].reshape(GMAX, expert_count, piece_rows, out_part)
    weights_mine = lax.all_to_all(picked, "expert", split_axis=1, concat_axis=1, tiled=True)
    member_weights = weights_mine.reshape(GMAX, full_width, out_part)

    flat_rows = rows.reshape(-1, full_width)
    gram_sum = lax.dot_general(
        flat_rows, flat_rows, (((0,), (0,)), ((), ())), preferred_element_type=jnp.float32
    )
    ridge_term = damping * jnp.trace(gram_sum) / full_width + epsilon
    inverse = spd_inverse(gram_sum + ridge_term * jnp.eye(full_width, dtype=jnp.float32))

    projected = jnp.einsum(
        "rsf,rfd->rsd", rows, member_weights, preferred_element_type=jnp.float32
    ).astype(jnp.bfloat16)
    partial_value = lax.dot_general(
        flat_rows,
        projected.reshape(-1, out_part),
        (((0,), (0,)), ((), ())),
        preferred_element_type=jnp.float32,
    )
    merged = jnp.dot(
        inverse, partial_value, precision=HIGHEST, preferred_element_type=jnp.float32
    )
    return merged.astype(jnp.bfloat16).reshape(1, full_width, out_part)


def solution(mesh):
    return jax.shard_map(
        on_device,
        mesh=mesh,
        in_specs=(P("expert", None), P("expert", None, "mp"), P("expert", None, "mp"), P()),
        out_specs=P("expert", None, "mp"),
        check_vma=False,
    )
```

```python
import jax
import jax.numpy as jnp
from jax import lax
from jax.experimental import pallas as pl
from jax.experimental.pallas import tpu as pltpu
from jax.sharding import PartitionSpec as P

GMAX = 3
BLOCK = 128
PANEL = 8

damping = 0.1
epsilon = 1e-05
HIGHEST = lax.Precision.HIGHEST


def slot_rank(labels, label_count):
    count = labels.shape[0]
    onehot = labels[:, None] == jnp.arange(label_count, dtype=jnp.int32)[None, :]
    order = jnp.arange(count, dtype=jnp.int32)
    before = (order[None, :] < order[:, None]).astype(jnp.bfloat16)
    ahead = jnp.dot(before, onehot.astype(jnp.bfloat16), preferred_element_type=jnp.float32)
    return jnp.sum(jnp.where(onehot, ahead, 0.0), axis=1).astype(jnp.int32)


def invert_small(entry):
    size = len(entry)
    value = {(i, j): entry[i][j] for i in range(size) for j in range(i, size)}

    def get(i, j):
        return value[(min(i, j), max(i, j))]

    for k in range(0, size, 2):
        a, b, d = get(k, k), get(k, k + 1), get(k + 1, k + 1)
        scale = 1.0 / (a * d - b * b)
        a, b, d = a * scale, b * scale, d * scale
        others = [i for i in range(size) if i not in (k, k + 1)]
        scaled = {
            i: (get(i, k) * d - get(i, k + 1) * b, get(i, k + 1) * a - get(i, k) * b)
            for i in others
        }
        for i in others:
            for j in others:
                if i <= j:
                    value[(i, j)] = value[(i, j)] - (
                        scaled[i][0] * get(j, k) + scaled[i][1] * get(j, k + 1)
                    )
        for i in others:
            value[(min(i, k), max(i, k))] = scaled[i][0]
            value[(min(i, k + 1), max(i, k + 1))] = scaled[i][1]
        value[(k, k)], value[(k, k + 1)], value[(k + 1, k + 1)] = -d, b, -a
    return [[-get(i, j) for j in range(size)] for i in range(size)]


def tree_sum(terms):
    while len(terms) > 1:
        terms = [sum(terms[i : i + 2][1:], terms[i]) for i in range(0, len(terms), 2)]
    return terms[0]


def invert_tile(tile_ref):
    size = tile_ref.shape[0]
    full = (PANEL, size)
    lane = lax.broadcasted_iota(jnp.int32, full, 1)
    sub = lax.broadcasted_iota(jnp.int32, full, 0)
    panels = size // PANEL
    group = [tile_ref[g * PANEL : (g + 1) * PANEL, :] for g in range(panels)]
    for p in range(panels):
        first = p * PANEL
        columns = [jnp.broadcast_to(group[p][:, first + j : first + j + 1], full) for j in range(PANEL)]
        entry = [
            [jnp.broadcast_to(columns[j][i : i + 1, :], full) for j in range(PANEL)]
            for i in range(PANEL)
        ]
        inverse = invert_small(entry)
        own = [inverse[0][j] for j in range(PANEL)]
        for i in range(1, PANEL):
            own = [jnp.where(sub == i, inverse[i][j], own[j]) for j in range(PANEL)]
        row = [jnp.broadcast_to(group[p][j : j + 1, :], full) for j in range(PANEL)]
        scaled = tree_sum([own[j] * row[j] for j in range(PANEL)])
        for j in range(PANEL):
            scaled = jnp.where(lane == first + j, own[j], scaled)
        spread = [jnp.broadcast_to(scaled[j : j + 1, :], full) for j in range(PANEL)]
        pivots = (lane >= first) & (lane < first + PANEL)
        order = [(p + 1 + g) % panels for g in range(panels - 1)]
        for g in order:
            here = group[g]
            group[g] = jnp.where(pivots, 0.0, here) - tree_sum(
                [
                    jnp.broadcast_to(here[:, first + j : first + j + 1], full) * spread[j]
                    for j in range(PANEL)
                ]
            )
        group[p] = scaled
    for g in range(panels):
        tile_ref[g * PANEL : (g + 1) * PANEL, :] = group[g]


def inverse_kernel(a_ref, o_ref, s_ref, d_ref):
    size = a_ref.shape[0]
    o_ref[...] = a_ref[...]
    tiles = size // BLOCK

    def eliminate(step, carry):
        span = pl.ds(pl.multiple_of(step * BLOCK, BLOCK), BLOCK)
        d_ref[...] = o_ref[span, span]
        invert_tile(d_ref)
        inverse = d_ref[...]
        s_ref[...] = jnp.dot(
            inverse, o_ref[span, :], precision=HIGHEST, preferred_element_type=jnp.float32
        )
        s_ref[:, span] = inverse

        def update(tile, inner):
            here = pl.ds(pl.multiple_of(tile * BLOCK, BLOCK), BLOCK)
            column = o_ref[here, span]
            o_ref[here, span] = jnp.zeros((BLOCK, BLOCK), jnp.float32)
            o_ref[here, :] = o_ref[here, :] - jnp.dot(
                column, s_ref[...], precision=HIGHEST, preferred_element_type=jnp.float32
            )
            return inner

        lax.fori_loop(0, tiles, update, 0)
        o_ref[span, :] = s_ref[...]
        return carry

    lax.fori_loop(0, tiles, eliminate, 0)


def spd_inverse(system):
    size = system.shape[0]
    return pl.pallas_call(
        inverse_kernel,
        out_shape=jax.ShapeDtypeStruct(system.shape, jnp.float32),
        in_specs=[pl.BlockSpec(memory_space=pltpu.VMEM)],
        out_specs=pl.BlockSpec(memory_space=pltpu.VMEM),
        scratch_shapes=[
            pltpu.VMEM((BLOCK, size), jnp.float32),
            pltpu.VMEM((BLOCK, BLOCK), jnp.float32),
        ],
        compiler_params=pltpu.CompilerParams(vmem_limit_bytes=24 << 20),
        cost_estimate=pl.CostEstimate(
            flops=50 * size**3, bytes_accessed=8 * size * size, transcendentals=0
        ),
    )(system)


def exchange_kernel(outgoing, weights, rows, pieces, sems_row, sems_weight, sems_gather, sems_own):
    me, ranks = lax.axis_index("expert"), lax.axis_size("expert")
    part, parts = lax.axis_index("mp"), lax.axis_size("mp")
    width = outgoing.shape[-1]
    piece_rows = pieces.shape[2]
    barrier = pltpu.get_barrier_semaphore()
    for hop in range(1, ranks):
        pl.semaphore_signal(barrier, inc=1, device_id={"expert": lax.rem(me + hop, ranks)})
    for hop in range(1, parts):
        pl.semaphore_signal(barrier, inc=1, device_id={"mp": lax.rem(part + hop, parts)})
    pl.semaphore_wait(barrier, ranks + parts - 2)

    mine = pl.ds(pl.multiple_of(part * width, width), width)

    def weight_rows(owner):
        return weights.at[:, pl.ds(pl.multiple_of(owner * piece_rows, piece_rows), piece_rows), :]

    row_copies, weight_copies, gather_copies = [], [], []
    for hop in range(1, ranks):
        peer = lax.rem(me + hop, ranks)
        row_copies.append(
            pltpu.make_async_remote_copy(
                src_ref=outgoing.at[peer],
                dst_ref=rows.at[:, me, :, mine],
                send_sem=sems_row.at[0, hop],
                recv_sem=sems_row.at[1, hop],
                device_id={"expert": peer},
            )
        )
        weight_copies.append(
            pltpu.make_async_remote_copy(
                src_ref=weight_rows(peer),
                dst_ref=pieces.at[me],
                send_sem=sems_weight.at[0, hop],
                recv_sem=sems_weight.at[1, hop],
                device_id={"expert": peer},
            )
        )
    own_rows = pltpu.make_async_copy(outgoing.at[me], rows.at[:, me, :, mine], sems_own.at[0])
    own_weights = pltpu.make_async_copy(weight_rows(me), pieces.at[me], sems_own.at[1])
    own_rows.start()
    for copy in row_copies:
        copy.start()
    for copy in weight_copies:
        copy.start()
    own_weights.start()
    own_rows.wait()
    for copy in row_copies:
        copy.wait()
    for hop in range(1, parts):
        gather_copies.append(
            pltpu.make_async_remote_copy(
                src_ref=rows.at[:, :, :, mine],
                dst_ref=rows.at[:, :, :, mine],
                send_sem=sems_gather.at[0, hop],
                recv_sem=sems_gather.at[1, hop],
                device_id={"mp": lax.rem(part + hop, parts)},
            )
        )
    for copy in gather_copies:
        copy.start()
    own_weights.wait()
    for copy in weight_copies:
        copy.wait()
    for copy in gather_copies:
        copy.wait()


def exchange(outgoing, weights, ranks, parts):
    _, members, cap, width = outgoing.shape
    local_count, full_width, out_part = weights.shape
    anywhere = pl.BlockSpec(memory_space=pl.ANY)
    return pl.pallas_call(
        exchange_kernel,
        out_shape=(
            jax.ShapeDtypeStruct((members, ranks, cap, width * parts), outgoing.dtype),
            jax.ShapeDtypeStruct(
                (ranks, local_count, full_width // ranks, out_part), weights.dtype
            ),
        ),
        in_specs=[anywhere, anywhere],
        out_specs=(anywhere, anywhere),
        scratch_shapes=[
            pltpu.SemaphoreType.DMA((2, ranks)),
            pltpu.SemaphoreType.DMA((2, ranks)),
            pltpu.SemaphoreType.DMA((2, parts)),
            pltpu.SemaphoreType.DMA((2,)),
        ],
        compiler_params=pltpu.CompilerParams(collective_id=0, has_side_effects=True),
    )(outgoing, weights)


def on_device(routes, routed_hidden, down_proj, merge_group):
    expert_count = lax.axis_size("expert")
    local_count = down_proj.shape[0]
    expert_total = local_count * expert_count
    tok_count, top_count = routes.shape
    hidden_part = routed_hidden.shape[2]
    full_width = down_proj.shape[1]
    out_part = down_proj.shape[2]
    slot_cap = 3 * tok_count * top_count // (2 * expert_total)
    row_count = tok_count * top_count
    piece_rows = full_width // expert_count

    experts = jnp.arange(expert_total, dtype=jnp.int32)
    member_rank = slot_rank(merge_group, expert_count)
    first_slot = (merge_group * GMAX + member_rank) * slot_cap
    targets = routes.reshape(row_count)
    position = slot_rank(targets, expert_total)
    slot_index = position + jnp.sum(
        jnp.where(targets[:, None] == experts[None, :], first_slot[None, :], 0), axis=1
    )
    slots = jnp.arange(GMAX * expert_count * slot_cap, dtype=jnp.int32)
    chosen = (slots[:, None] == slot_index[None, :]).astype(jnp.bfloat16)
    outgoing = jnp.dot(
        chosen,
        routed_hidden.reshape(row_count, hidden_part),
        preferred_element_type=jnp.float32,
    ).astype(jnp.bfloat16)
    outgoing = outgoing.reshape(expert_count, GMAX, slot_cap, hidden_part)
    rows, pieces = exchange(outgoing, down_proj, expert_count, lax.axis_size("mp"))
    rows = rows.reshape(GMAX, expert_count * slot_cap, full_width)

    table = jnp.arange(GMAX * expert_count, dtype=jnp.int32)
    place = merge_group * GMAX + member_rank
    members = jnp.sum(jnp.where(table[:, None] == place[None, :], experts[None, :], 0), axis=1)
    picked = pieces.reshape(expert_total, piece_rows, out_part)[members]
    picked = picked.reshape(expert_count, GMAX, piece_rows, out_part)
    arrived = lax.all_to_all(picked, "expert", split_axis=0, concat_axis=0, tiled=True)
    member_weights = arrived.transpose(1, 0, 2, 3).reshape(GMAX, full_width, out_part)

    flat_rows = rows.reshape(-1, full_width)
    gram_sum = lax.dot_general(
        flat_rows, flat_rows, (((0,), (0,)), ((), ())), preferred_element_type=jnp.float32
    )
    ridge_term = damping * jnp.trace(gram_sum) / full_width + epsilon
    inverse = spd_inverse(gram_sum + ridge_term * jnp.eye(full_width, dtype=jnp.float32))

    projected = jnp.einsum(
        "rsf,rfd->rsd", rows, member_weights, preferred_element_type=jnp.float32
    ).astype(jnp.bfloat16)
    partial_value = lax.dot_general(
        flat_rows,
        projected.reshape(-1, out_part),
        (((0,), (0,)), ((), ())),
        preferred_element_type=jnp.float32,
    )
    merged = jnp.dot(
        inverse, partial_value, precision=HIGHEST, preferred_element_type=jnp.float32
    )
    return merged.astype(jnp.bfloat16).reshape(1, full_width, out_part)


def solution(mesh):
    return jax.shard_map(
        on_device,
        mesh=mesh,
        in_specs=(P("expert", None), P("expert", None, "mp"), P("expert", None, "mp"), P()),
        out_specs=P("expert", None, "mp"),
        check_vma=False,
    )
```

```python
import jax
import jax.numpy as jnp
from jax import lax
from jax.experimental import pallas as pl
from jax.experimental.pallas import tpu as pltpu
from jax.sharding import PartitionSpec as P

GMAX = 3
BLOCK = 128
PANEL = 8

damping = 0.1
epsilon = 1e-05
HIGHEST = lax.Precision.HIGHEST


def slot_rank(labels, label_count):
    count = labels.shape[0]
    onehot = labels[:, None] == jnp.arange(label_count, dtype=jnp.int32)[None, :]
    order = jnp.arange(count, dtype=jnp.int32)
    before = (order[None, :] < order[:, None]).astype(jnp.bfloat16)
    ahead = jnp.dot(before, onehot.astype(jnp.bfloat16), preferred_element_type=jnp.float32)
    return jnp.sum(jnp.where(onehot, ahead, 0.0), axis=1).astype(jnp.int32)


def invert_small(entry):
    size = len(entry)
    value = {(i, j): entry[i][j] for i in range(size) for j in range(i, size)}

    def get(i, j):
        return value[(min(i, j), max(i, j))]

    for k in range(0, size, 2):
        a, b, d = get(k, k), get(k, k + 1), get(k + 1, k + 1)
        scale = 1.0 / (a * d - b * b)
        a, b, d = a * scale, b * scale, d * scale
        others = [i for i in range(size) if i not in (k, k + 1)]
        scaled = {
            i: (get(i, k) * d - get(i, k + 1) * b, get(i, k + 1) * a - get(i, k) * b)
            for i in others
        }
        for i in others:
            for j in others:
                if i <= j:
                    value[(i, j)] = value[(i, j)] - (
                        scaled[i][0] * get(j, k) + scaled[i][1] * get(j, k + 1)
                    )
        for i in others:
            value[(min(i, k), max(i, k))] = scaled[i][0]
            value[(min(i, k + 1), max(i, k + 1))] = scaled[i][1]
        value[(k, k)], value[(k, k + 1)], value[(k + 1, k + 1)] = -d, b, -a
    return [[-get(i, j) for j in range(size)] for i in range(size)]


def tree_sum(terms):
    while len(terms) > 1:
        terms = [sum(terms[i : i + 2][1:], terms[i]) for i in range(0, len(terms), 2)]
    return terms[0]


def invert_tile(tile_ref):
    size = tile_ref.shape[0]
    full = (PANEL, size)
    lane = lax.broadcasted_iota(jnp.int32, full, 1)
    sub = lax.broadcasted_iota(jnp.int32, full, 0)
    panels = size // PANEL
    group = [tile_ref[g * PANEL : (g + 1) * PANEL, :] for g in range(panels)]
    for p in range(panels):
        first = p * PANEL
        columns = [jnp.broadcast_to(group[p][:, first + j : first + j + 1], full) for j in range(PANEL)]
        entry = [
            [jnp.broadcast_to(columns[j][i : i + 1, :], full) for j in range(PANEL)]
            for i in range(PANEL)
        ]
        inverse = invert_small(entry)
        own = [inverse[0][j] for j in range(PANEL)]
        for i in range(1, PANEL):
            own = [jnp.where(sub == i, inverse[i][j], own[j]) for j in range(PANEL)]
        row = [jnp.broadcast_to(group[p][j : j + 1, :], full) for j in range(PANEL)]
        scaled = tree_sum([own[j] * row[j] for j in range(PANEL)])
        for j in range(PANEL):
            scaled = jnp.where(lane == first + j, own[j], scaled)
        spread = [jnp.broadcast_to(scaled[j : j + 1, :], full) for j in range(PANEL)]
        pivots = (lane >= first) & (lane < first + PANEL)
        order = [(p + 1 + g) % panels for g in range(panels - 1)]
        for g in order:
            here = group[g]
            group[g] = jnp.where(pivots, 0.0, here) - tree_sum(
                [
                    jnp.broadcast_to(here[:, first + j : first + j + 1], full) * spread[j]
                    for j in range(PANEL)
                ]
            )
        group[p] = scaled
    for g in range(panels):
        tile_ref[g * PANEL : (g + 1) * PANEL, :] = group[g]


def inverse_kernel(a_ref, o_ref, s_ref, d_ref):
    size = a_ref.shape[0]
    o_ref[...] = a_ref[...]
    tiles = size // BLOCK

    def eliminate(step, carry):
        span = pl.ds(pl.multiple_of(step * BLOCK, BLOCK), BLOCK)
        d_ref[...] = o_ref[span, span]
        invert_tile(d_ref)
        inverse = d_ref[...]
        s_ref[...] = jnp.dot(
            inverse, o_ref[span, :], precision=HIGHEST, preferred_element_type=jnp.float32
        )
        s_ref[:, span] = inverse

        def update(tile, inner):
            here = pl.ds(pl.multiple_of(tile * BLOCK, BLOCK), BLOCK)
            column = o_ref[here, span]
            o_ref[here, span] = jnp.zeros((BLOCK, BLOCK), jnp.float32)
            o_ref[here, :] = o_ref[here, :] - jnp.dot(
                column, s_ref[...], precision=HIGHEST, preferred_element_type=jnp.float32
            )
            return inner

        lax.fori_loop(0, tiles, update, 0)
        o_ref[span, :] = s_ref[...]
        return carry

    lax.fori_loop(0, tiles, eliminate, 0)


def spd_inverse(system):
    size = system.shape[0]
    return pl.pallas_call(
        inverse_kernel,
        out_shape=jax.ShapeDtypeStruct(system.shape, jnp.float32),
        in_specs=[pl.BlockSpec(memory_space=pltpu.VMEM)],
        out_specs=pl.BlockSpec(memory_space=pltpu.VMEM),
        scratch_shapes=[
            pltpu.VMEM((BLOCK, size), jnp.float32),
            pltpu.VMEM((BLOCK, BLOCK), jnp.float32),
        ],
        compiler_params=pltpu.CompilerParams(vmem_limit_bytes=24 << 20),
        cost_estimate=pl.CostEstimate(
            flops=50 * size**3, bytes_accessed=8 * size * size, transcendentals=0
        ),
    )(system)


def exchange_kernel(outgoing, weights, rows, pieces, sems_row, sems_weight, sems_gather, sems_own):
    me, ranks = lax.axis_index("expert"), lax.axis_size("expert")
    part, parts = lax.axis_index("mp"), lax.axis_size("mp")
    width = outgoing.shape[-1]
    piece_rows = pieces.shape[2]
    barrier = pltpu.get_barrier_semaphore()
    for hop in range(1, ranks):
        pl.semaphore_signal(barrier, inc=1, device_id={"expert": lax.rem(me + hop, ranks)})
    for hop in range(1, parts):
        pl.semaphore_signal(barrier, inc=1, device_id={"mp": lax.rem(part + hop, parts)})
    pl.semaphore_wait(barrier, ranks + parts - 2)

    mine = pl.ds(pl.multiple_of(part * width, width), width)

    def weight_rows(owner):
        return weights.at[:, pl.ds(pl.multiple_of(owner * piece_rows, piece_rows), piece_rows), :]

    row_copies, weight_copies, gather_copies = [], [], []
    for hop in range(1, ranks):
        peer = lax.rem(me + hop, ranks)
        row_copies.append(
            pltpu.make_async_remote_copy(
                src_ref=outgoing.at[peer],
                dst_ref=rows.at[:, me, :, mine],
                send_sem=sems_row.at[0, hop],
                recv_sem=sems_row.at[1, hop],
                device_id={"expert": peer},
            )
        )
        weight_copies.append(
            pltpu.make_async_remote_copy(
                src_ref=weight_rows(peer),
                dst_ref=pieces.at[me],
                send_sem=sems_weight.at[0, hop],
                recv_sem=sems_weight.at[1, hop],
                device_id={"expert": peer},
            )
        )
    own_rows = pltpu.make_async_copy(outgoing.at[me], rows.at[:, me, :, mine], sems_own.at[0])
    own_weights = pltpu.make_async_copy(weight_rows(me), pieces.at[me], sems_own.at[1])
    own_rows.start()
    for copy in row_copies:
        copy.start()
    for copy in weight_copies:
        copy.start()
    own_weights.start()
    own_rows.wait()
    for copy in row_copies:
        copy.wait()
    for hop in range(1, parts):
        gather_copies.append(
            pltpu.make_async_remote_copy(
                src_ref=rows.at[:, :, :, mine],
                dst_ref=rows.at[:, :, :, mine],
                send_sem=sems_gather.at[0, hop],
                recv_sem=sems_gather.at[1, hop],
                device_id={"mp": lax.rem(part + hop, parts)},
            )
        )
    for copy in gather_copies:
        copy.start()
    own_weights.wait()
    for copy in weight_copies:
        copy.wait()
    for copy in gather_copies:
        copy.wait()


def exchange(outgoing, weights, ranks, parts):
    _, members, cap, width = outgoing.shape
    local_count, full_width, out_part = weights.shape
    anywhere = pl.BlockSpec(memory_space=pl.ANY)
    return pl.pallas_call(
        exchange_kernel,
        out_shape=(
            jax.ShapeDtypeStruct((members, ranks, cap, width * parts), outgoing.dtype),
            jax.ShapeDtypeStruct(
                (ranks, local_count, full_width // ranks, out_part), weights.dtype
            ),
        ),
        in_specs=[anywhere, anywhere],
        out_specs=(anywhere, anywhere),
        scratch_shapes=[
            pltpu.SemaphoreType.DMA((2, ranks)),
            pltpu.SemaphoreType.DMA((2, ranks)),
            pltpu.SemaphoreType.DMA((2, parts)),
            pltpu.SemaphoreType.DMA((2,)),
        ],
        compiler_params=pltpu.CompilerParams(collective_id=0, has_side_effects=True),
    )(outgoing, weights)


def on_device(routes, routed_hidden, down_proj, merge_group):
    expert_count = lax.axis_size("expert")
    local_count = down_proj.shape[0]
    expert_total = local_count * expert_count
    tok_count, top_count = routes.shape
    hidden_part = routed_hidden.shape[2]
    full_width = down_proj.shape[1]
    out_part = down_proj.shape[2]
    slot_cap = 3 * tok_count * top_count // (2 * expert_total)
    row_count = tok_count * top_count
    piece_rows = full_width // expert_count

    experts = jnp.arange(expert_total, dtype=jnp.int32)
    member_rank = slot_rank(merge_group, expert_count)
    first_slot = (merge_group * GMAX + member_rank) * slot_cap
    targets = routes.reshape(row_count)
    position = slot_rank(targets, expert_total)
    slot_index = position + jnp.sum(
        jnp.where(targets[:, None] == experts[None, :], first_slot[None, :], 0), axis=1
    )
    slots = jnp.arange(GMAX * expert_count * slot_cap, dtype=jnp.int32)
    chosen = (slots[:, None] == slot_index[None, :]).astype(jnp.bfloat16)
    outgoing = jnp.dot(
        chosen,
        routed_hidden.reshape(row_count, hidden_part),
        preferred_element_type=jnp.float32,
    ).astype(jnp.bfloat16)
    outgoing = outgoing.reshape(expert_count, GMAX, slot_cap, hidden_part)
    rows, pieces = exchange(outgoing, down_proj, expert_count, lax.axis_size("mp"))
    rows = rows.reshape(GMAX, expert_count * slot_cap, full_width)

    table = jnp.arange(GMAX * expert_count, dtype=jnp.int32)
    place = merge_group * GMAX + member_rank
    members = jnp.sum(jnp.where(table[:, None] == place[None, :], experts[None, :], 0), axis=1)
    picked = pieces.reshape(expert_total, piece_rows, out_part)[members]
    picked = picked.reshape(expert_count, GMAX, piece_rows, out_part)
    arrived = lax.all_to_all(picked, "expert", split_axis=0, concat_axis=0, tiled=True)
    member_weights = arrived.transpose(1, 0, 2, 3).reshape(GMAX, full_width, out_part)

    flat_rows = rows.reshape(-1, full_width)
    gram_sum = lax.dot_general(
        flat_rows, flat_rows, (((0,), (0,)), ((), ())), preferred_element_type=jnp.float32
    )
    ridge_term = damping * jnp.trace(gram_sum) / full_width + epsilon
    inverse = spd_inverse(gram_sum + ridge_term * jnp.eye(full_width, dtype=jnp.float32))

    projected = jnp.einsum(
        "rsf,rfd->rsd", rows, member_weights, preferred_element_type=jnp.float32
    ).astype(jnp.bfloat16)
    partial_value = lax.dot_general(
        flat_rows,
        projected.reshape(-1, out_part),
        (((0,), (0,)), ((), ())),
        preferred_element_type=jnp.float32,
    )
    merged = jnp.dot(
        inverse, partial_value, precision=lax.Precision.HIGH, preferred_element_type=jnp.float32
    )
    return merged.astype(jnp.bfloat16).reshape(1, full_width, out_part)


def solution(mesh):
    return jax.shard_map(
        on_device,
        mesh=mesh,
        in_specs=(P("expert", None), P("expert", None, "mp"), P("expert", None, "mp"), P()),
        out_specs=P("expert", None, "mp"),
        check_vma=False,
    )
```
